32 devices in a mesh: row: 4 (over z), col: 8 (over y, x, core).
Axes of the slice: x: 2, y: 2, z: 4, core: 2. Of those that a mesh axis runs over, the one named last changes fastest.
Arguments:
- tokens: bfloat16 [512, 4096], P('row', 'col'), may hold values from -6 to 6
- cotangent: bfloat16 [512, 4096], P('row', 'col'), may hold values from -6 to 6
- gate_weight: bfloat16 [4096, 16384], P('row', 'col'), may hold values from -0.1875 to 0.1875
- up_weight: bfloat16 [4096, 16384], P('row', 'col'), may hold values from -0.1875 to 0.1875
- down_weight: bfloat16 [16384, 4096], P('col', 'row'), may hold values from -0.09375 to 0.09375
- gate_mask: int32 [32, 128], P('row', 'col'), may hold values from 0 to 1, as said below
- up_mask: int32 [32, 128], P('row', 'col'), may hold values from 0 to 1, as said below
- down_mask: int32 [128, 32], P('col', 'row'), may hold values from 0 to 1, as said below
Outputs:
- output: bfloat16 [512, 4096], P('row', 'col')
- grad_tokens: bfloat16 [512, 4096], P('row', 'col')
The draws below stay inside these ranges and needn't reach their ends.
Inputs may be any that keep to these rules, and one draw needn't show every extreme that they name: `gate_mask`: cut into aligned tiles of 8 x 16 entries (one device's shard), no tile holds more than 96 ones and some tile holds exactly 96. `up_mask`: cut into aligned tiles of 8 x 16 entries (one device's shard), no tile holds more than 96 ones and some tile holds exactly 96. `down_mask`: cut into aligned tiles of 16 x 8 entries (one device's shard), no tile holds more than 96 ones and some tile holds exactly 96.
All inputs are finite; a program needn't handle non-finite values.
Results may differ from the reference program's by a relative error of at most 0.015.
Values may be sent and summed in bfloat16 or wider, within the bound.
A program may use at most 192 MiB of HBM per device.

```python
import jax
import jax.numpy as jnp
from jax import lax

BLOCK = 128
D = 4096
FF = 16384
TOKENS = 512
CAP = 96
N_ROW = 4
N_COL = 8


def mask_draw(key, row_blocks, col_blocks, row_parts, col_parts):
    per_row = row_blocks // row_parts
    per_col = col_blocks // col_parts
    shard_count = row_parts * col_parts
    shard_blocks = per_row * per_col
    key_fullest, key_counts, key_order = jax.random.split(key, 3)
    fullest = jax.random.randint(key_fullest, (), 0, shard_count)
    counts = jax.random.randint(key_counts, (shard_count,), shard_blocks // 4, CAP + 1)
    counts = jnp.where(jnp.arange(shard_count) == fullest, CAP, counts)
    scores = jax.random.randint(key_order, (shard_count, shard_blocks), 0, 1 << 20)
    scores = scores * shard_blocks + jnp.arange(shard_blocks, dtype=jnp.int32)[None, :]
    rank_order = jnp.argsort(jnp.argsort(scores, axis=1), axis=1)
    kept_mask = (rank_order < counts[:, None]).astype(jnp.int32)
    kept_mask = kept_mask.reshape(row_parts, col_parts, per_row, per_col)
    kept_mask = kept_mask.transpose(0, 2, 1, 3).reshape(row_blocks, col_blocks)
    return kept_mask


def draw_gate_mask(key, part):
    return mask_draw(jax.random.fold_in(key, 11), D // BLOCK, FF // BLOCK, N_ROW, N_COL)


def draw_up_mask(key, part):
    return mask_draw(jax.random.fold_in(key, 23), D // BLOCK, FF // BLOCK, N_ROW, N_COL)


def draw_down_mask(key, part):
    return mask_draw(jax.random.fold_in(key, 37), FF // BLOCK, D // BLOCK, N_COL, N_ROW)


def spiked(result, own_key, source, target, parts, factor):
    owner, partner = [(jnp.arange(result.shape[dim]) // (result.shape[dim] // parts)).reshape([-1 if axis == dim else 1 for axis in range(result.ndim)]) for dim in (source, target)]
    chosen = jax.random.permutation(own_key, parts)[partner]
    strong = (owner == chosen) | (owner == (partner + parts // 2) % parts)
    return jnp.where(strong, factor * result, result)


def block_scale(stream_key, dims, cuts, least, high):
    level, own = 1.0, jax.random.fold_in(stream_key, 6)
    for position, parts in cuts:
        draws = jnp.exp(jax.random.uniform(jax.random.fold_in(own, position), (parts,), jnp.float32, least / len(cuts), high / len(cuts)))
        level = level * jnp.repeat(draws, dims[position] // parts).reshape([-1 if axis == position else 1 for axis in range(len(dims))])
    return level


def noise(rng, extent, scale, most, shards=(), held_as=jnp.bfloat16):
    drawn = scale * jax.random.normal(rng, extent, jnp.float32)
    if shards:
        drawn = drawn * block_scale(rng, extent, shards, -0.22, 0.18)
    return jnp.clip(drawn, -most, most).astype(held_as)


def noise_with(own_key, extent, deviation, limit, cuts, heavy, kind=jnp.bfloat16):
    values = deviation * jax.random.normal(own_key, extent, jnp.float32)
    if cuts:
        values = values * block_scale(own_key, extent, cuts, -0.22, 0.18)
    return jnp.clip(spiked(values, jax.random.fold_in(own_key, 3), *heavy), -limit, limit).astype(kind)


def setup_inputs(seed: int = 0) -> dict:
    streams_of = jax.random.split(jax.random.key(seed), 9)
    tokens = noise(streams_of[0], (TOKENS, D), 1.0, 6.0, ((0, 4), (1, 8)))
    cotangent = noise(streams_of[1], (TOKENS, D), 1.0, 6.0, ((0, 4), (1, 8)))
    gate_weight = noise_with(streams_of[2], (D, FF), (D // 2) ** -0.5, 0.1875, ((0, 4), (1, 8)), (1, 0, 8, 2.0))
    up_weight = noise_with(streams_of[3], (D, FF), (D // 2) ** -0.5, 0.1875, ((0, 4), (1, 8)), (1, 0, 8, 2.0))
    down_weight = noise_with(streams_of[4], (FF, D), (FF // 2) ** -0.5, 0.09375, ((0, 8), (1, 4)), (0, 1, 8, 2.0))
    gate_mask = draw_gate_mask(jax.random.fold_in(streams_of[8], 71), 0)
    up_mask = draw_up_mask(jax.random.fold_in(streams_of[8], 71), 0)
    down_mask = draw_down_mask(jax.random.fold_in(streams_of[8], 71), 0)
    return dict(tokens=tokens, cotangent=cotangent, gate_weight=gate_weight, up_weight=up_weight, down_weight=down_weight, gate_mask=gate_mask, up_mask=up_mask, down_mask=down_mask)


def masked(weight, block_mask):
    row_count, col_count = block_mask.shape
    shaped = weight.reshape(row_count, BLOCK, col_count, BLOCK)
    scaled = shaped * block_mask.astype(weight.dtype)[:, None, :, None]
    return scaled.reshape(weight.shape)


def reference(tokens, cotangent, gate_weight, up_weight, down_weight, gate_mask, up_mask, down_mask):
    gate_eff = masked(gate_weight, gate_mask)
    up_eff = masked(up_weight, up_mask)
    down_eff = masked(down_weight, down_mask)
    gate = jnp.dot(tokens, gate_eff, preferred_element_type=jnp.float32)
    up = jnp.dot(tokens, up_eff, preferred_element_type=jnp.float32)
    sigma = jax.nn.sigmoid(gate)
    silu_gate = gate * sigma
    hidden = (silu_gate * up).astype(jnp.bfloat16)
    grad_hidden = jnp.dot(cotangent, down_eff.T, preferred_element_type=jnp.float32)
    grad_gate = (grad_hidden * up * sigma * (1.0 + gate * (1.0 - sigma))).astype(jnp.bfloat16)
    grad_up = (grad_hidden * silu_gate).astype(jnp.bfloat16)
    span = FF // N_COL

    def add_group(carry, group):
        out_total, grad_total = carry
        start = group * span
        hidden_share = lax.dynamic_slice_in_dim(hidden, start, span, 1)
        down_rows = lax.dynamic_slice_in_dim(down_eff, start, span, 0)
        out_part = jnp.dot(hidden_share, down_rows, preferred_element_type=jnp.float32).astype(jnp.bfloat16)
        out_part = lax.optimization_barrier(out_part).astype(jnp.float32)
        gate_share = lax.dynamic_slice_in_dim(grad_gate, start, span, 1)
        up_share = lax.dynamic_slice_in_dim(grad_up, start, span, 1)
        gate_cols = lax.dynamic_slice_in_dim(gate_eff, start, span, 1)
        up_cols = lax.dynamic_slice_in_dim(up_eff, start, span, 1)
        grad_part = jnp.dot(gate_share, gate_cols.T, preferred_element_type=jnp.float32)
        grad_part = grad_part + jnp.dot(up_share, up_cols.T, preferred_element_type=jnp.float32)
        grad_part = lax.optimization_barrier(grad_part.astype(jnp.bfloat16)).astype(jnp.float32)
        return (out_total + out_part, grad_total + grad_part), None

    zeros = jnp.zeros(tokens.shape, jnp.float32)
    groups = jnp.arange(N_COL, dtype=jnp.int32)
    (out_total, grad_total), unused = lax.scan(add_group, (zeros, zeros), groups)
    return out_total.astype(jnp.bfloat16), grad_total.astype(jnp.bfloat16)
```

```python
import functools

import jax
import jax.numpy as jnp
from jax import lax
from jax.experimental import pallas as pl
from jax.experimental.pallas import tpu as pltpu
from jax.sharding import PartitionSpec as P

BLOCK = 128
TOKEN_BLOCK = 64
WIDTH = 256
LAG = 3
CONTRACT = (((1,), (1,)), ((), ()))
MESH_ID = pl.DeviceIdType.MESH
bf16, f32 = jnp.bfloat16, jnp.float32


def remote(src, dst, send, recv, row, col):
    return pltpu.make_async_remote_copy(
        src_ref=src, dst_ref=dst, send_sem=send, recv_sem=recv,
        device_id={"row": row, "col": col}, device_id_type=MESH_ID,
    )


def await_bytes(ref, sem):
    pltpu.make_async_copy(ref, ref, sem).wait()


def layer_kernel(
    rows, cols, tok_ref, cot_ref, wg_hbm, wu_hbm, wd_hbm, gm_ref, um_ref, dm_ref, out_ref, grad_ref,
    wg, wu, wd, panel, own, sums, acc, pout, land, total, result,
    w_sem, ch_send, ch_recv, src_send, pan_recv, root_send, sib_send, rs_send, rs_recv, fin_send, fin_recv,
):
    row, col = lax.axis_index("row"), lax.axis_index("col")
    last = rows - 1
    per = cols // rows
    chip, core = col // per, col % per
    blocks, _, _, size, feats = panel.shape
    slices, _, width = wg.shape
    subs = blocks // rows
    chunks = blocks * slices
    _, reducers, piece, _ = pout.shape
    split = reducers // (2 * per)

    low = row < rows // 2
    near, far = jnp.where(low, 0, 1), jnp.where(low, 1, 0)
    near_pos, far_pos = jnp.minimum(row, last - row), jnp.maximum(row, last - row)
    near_next = jnp.where(low, row + 1, row - 1)
    far_next = jnp.clip(jnp.where(low, row - 1, row + 1), 0, last)

    def load(j):
        span = pl.ds(pl.multiple_of(j * width, width), width)
        return (
            pltpu.make_async_copy(wg_hbm.at[:, span], wg.at[j], w_sem.at[0, j]),
            pltpu.make_async_copy(wu_hbm.at[:, span], wu.at[j], w_sem.at[1, j]),
            pltpu.make_async_copy(wd_hbm.at[span, :], wd.at[j], w_sem.at[2, j]),
        )

    def load_start(j, carry):
        for copy in load(j):
            copy.start()
        return carry

    lax.fori_loop(0, slices, load_start, 0)

    barrier = pltpu.get_barrier_semaphore()

    def greet(i, carry):
        @pl.when(i != row * cols + col)
        def _():
            pl.semaphore_signal(
                barrier, inc=1, device_id={"row": i // cols, "col": i % cols}, device_id_type=MESH_ID
            )
        return carry

    lax.fori_loop(0, rows * cols, greet, 0)
    pl.semaphore_wait(barrier, rows * cols - 1)

    def prune(j):
        for copy in load(j):
            copy.wait()
        for i in range(wg.shape[1] // BLOCK):
            for n in range(width // BLOCK):
                at = j * (width // BLOCK) + n
                feat, hid = slice(i * BLOCK, (i + 1) * BLOCK), slice(n * BLOCK, (n + 1) * BLOCK)
                wg[j, feat, hid] = wg[j, feat, hid] * jnp.full((BLOCK, BLOCK), gm_ref[i, at].astype(f32)).astype(bf16)
                wu[j, feat, hid] = wu[j, feat, hid] * jnp.full((BLOCK, BLOCK), um_ref[i, at].astype(f32)).astype(bf16)
                wd[j, hid, feat] = wd[j, hid, feat] * jnp.full((BLOCK, BLOCK), dm_ref[at, i].astype(f32)).astype(bf16)

    def source_copies(t):
        span = pl.ds(pl.multiple_of((t % subs) * size, size), size)
        return [
            remote(
                ref.at[span, :], panel.at[t, core, i], src_send.at[t % subs, i], pan_recv.at[t, core], chip, col
            )
            for i, ref in enumerate((tok_ref, cot_ref))
        ]

    def source(t):
        @pl.when((row == t // subs) & (chip == row))
        def _():
            span = pl.ds(pl.multiple_of((t % subs) * size, size), size)
            panel[t, core, 0] = tok_ref[span, :]
            panel[t, core, 1] = cot_ref[span, :]

        @pl.when((row == t // subs) & (chip != row))
        def _():
            for copy in source_copies(t):
                copy.start()

    def root_copies(t):
        return [
            remote(
                panel.at[t, core], panel.at[t, core], root_send.at[t, off - 1], pan_recv.at[t, core],
                row, lax.rem(chip + off, rows) * per + core,
            )
            for off in range(1, rows)
        ]

    def sibling_copies(t):
        return [
            remote(
                panel.at[t, core], panel.at[t, core], sib_send.at[t, off - 1], pan_recv.at[t, core],
                row, chip * per + lax.rem(core + off, per),
            )
            for off in range(1, per)
        ]

    def root(t):
        @pl.when(chip == row)
        def _():
            @pl.when(row != t // subs)
            def _():
                await_bytes(panel.at[t, core], pan_recv.at[t, core])

            for copy in root_copies(t) + sibling_copies(t):
                copy.start()

    def forward(t):
        @pl.when(chip != row)
        def _():
            await_bytes(panel.at[t, core], pan_recv.at[t, core])
            for copy in sibling_copies(t):
                copy.start()

    def arrive(t):
        for off in range(1, per):
            other = lax.rem(core + off, per)
            await_bytes(panel.at[t, other], pan_recv.at[t, other])

    def near_copy(k):
        return remote(
            sums.at[near, k], sums.at[near, k], ch_send.at[near, k], ch_recv.at[near, k], near_next, col
        )

    def far_copy(k):
        return remote(sums.at[far, k], sums.at[far, k], ch_send.at[far, k], ch_recv.at[far, k], far_next, col)

    def project(k):
        t, j = k // slices, k % slices

        @pl.when(k < slices)
        def _():
            prune(k)

        @pl.when(j == 0)
        def _():
            arrive(t)

        gate = up = grad = 0.0
        for h in range(per):
            feat = slice(h * feats, (h + 1) * feats)
            tok, cot = panel[t, h, 0], panel[t, h, 1]
            gate += jnp.dot(tok, wg[j, feat, :], preferred_element_type=f32)
            up += jnp.dot(tok, wu[j, feat, :], preferred_element_type=f32)
            grad += lax.dot_general(cot, wd[j, :, feat], CONTRACT, preferred_element_type=f32)
        own[k, 0] = gate
        own[k, 1] = up
        own[k, 2] = grad

    def pass_near(k):
        @pl.when(near_pos == 0)
        def _():
            sums[near, k] = own[k].astype(bf16)

        @pl.when(near_pos > 0)
        def _():
            near_copy(k).wait_recv()
            sums[near, k] = (own[k] + sums[near, k].astype(f32)).astype(bf16)

        near_copy(k).start()

    def pass_far(k):
        t, j = k // slices, k % slices
        far_copy(k).wait_recv()
        came = sums[far, k].astype(f32)
        whole = came + sums[near, k].astype(f32)

        @pl.when(far_pos < last)
        def _():
            sums[far, k] = (own[k] + came).astype(bf16)
            far_copy(k).start()

        gate, up, grad = whole[0], whole[1], whole[2]
        sigma = jax.nn.sigmoid(gate)
        silu = gate * sigma
        hidden = (silu * up).astype(bf16)
        grad_gate = (grad * up * sigma * (1.0 + gate * (1.0 - sigma))).astype(bf16)
        grad_up = (grad * silu).astype(bf16)

        @pl.when(j == 0)
        def _():
            acc[...] = jnp.zeros_like(acc)

        acc[0] += jnp.dot(hidden, wd[j], preferred_element_type=f32)
        acc[1] += lax.dot_general(grad_gate, wg[j], CONTRACT, preferred_element_type=f32) + lax.dot_general(
            grad_up, wu[j], CONTRACT, preferred_element_type=f32
        )

        @pl.when((j == slices // 2) & (t > 0))
        def _():
            combine(t - 1)

        @pl.when(j == slices - 1)
        def _():
            scatter(t)

    def scatter_copy(t, off):
        return remote(
            pout.at[t, lax.rem(col + off, cols) % reducers], land.at[t, cols - 1 - off], rs_send.at[t, off - 1],
            rs_recv.at[t], row, lax.rem(col + off, cols),
        )

    def scatter(t):
        for a in range(2):
            for h in range(per):
                for r in range(split):
                    pout[t, (a * per + h) * split + r] = acc[
                        a, r * piece : (r + 1) * piece, h * feats : (h + 1) * feats
                    ].astype(bf16)
        for off in range(1, cols):
            @pl.when(lax.rem(col + off, cols) < reducers)
            def _():
                scatter_copy(t, off).start()

    part = col % split
    half = (col // split) % per
    which = lax.rem(col // (split * per), 2)
    owner_col = row * per + half

    def give(t):
        span = pl.ds(pl.multiple_of((t % subs) * size + part * piece, piece), piece)
        return remote(
            total.at[t], result.at[which, span, :], fin_send.at[t], fin_recv.at[t % subs, which, part],
            t // subs, owner_col,
        )

    def combine(t):
        @pl.when(col < reducers)
        def _():
            await_bytes(land.at[t], rs_recv.at[t])
            value = pout[t, col % reducers].astype(f32)
            for i in range(cols - 1):
                value = value + land[t, i].astype(f32)
            mine = (row == t // subs) & (col == owner_col)

            @pl.when(mine)
            def _():
                span = pl.ds(pl.multiple_of((t % subs) * size + part * piece, piece), piece)
                result[which, span, :] = value.astype(bf16)

            @pl.when(jnp.logical_not(mine))
            def _():
                total[t] = value.astype(bf16)
                give(t).start()

    source(0)

    @pl.when(row == 0)
    def _():
        root(0)

    if blocks > 1:
        source(1)

    @pl.when(row != 0)
    def _():
        root(0)

    forward(0)
    project(0)

    def step(s, carry):
        t, j = s // slices, s % slices

        @pl.when((j == 0) & (t + 2 < blocks))
        def _():
            source(t + 2)

        @pl.when((j == slices // 4) & (t + 1 < blocks))
        def _():
            root(t + 1)

        @pl.when((j == slices * 5 // 8) & (t + 1 < blocks))
        def _():
            forward(t + 1)

        k_near = s - LAG * near_pos
        k_far = s - LAG * far_pos

        @pl.when((k_near >= 0) & (k_near < chunks))
        def _():
            pass_near(k_near)

        @pl.when((k_far >= 0) & (k_far < chunks))
        def _():
            pass_far(k_far)

        @pl.when(s + 1 < chunks)
        def _():
            project(s + 1)

        return carry

    lax.fori_loop(0, chunks + LAG * last, step, 0)
    combine(blocks - 1)

    def drain_chunk(k, carry):
        near_copy(k).wait_send()

        @pl.when(far_pos < last)
        def _():
            far_copy(k).wait_send()

        return carry

    lax.fori_loop(0, chunks, drain_chunk, 0)

    def drain_block(t, carry):
        @pl.when((row == t // subs) & (chip != row))
        def _():
            for copy in source_copies(t):
                copy.wait_send()

        @pl.when(chip == row)
        def _():
            for copy in root_copies(t):
                copy.wait_send()

        for copy in sibling_copies(t):
            copy.wait_send()

        for off in range(1, cols):
            @pl.when(lax.rem(col + off, cols) < reducers)
            def _():
                scatter_copy(t, off).wait_send()

        @pl.when((col < reducers) & jnp.logical_not((row == t // subs) & (col == owner_col)))
        def _():
            give(t).wait_send()

        return carry

    lax.fori_loop(0, blocks, drain_block, 0)

    for s in range(subs):
        for a in range(2):
            for r in range(split):
                @pl.when((row != chip) | (col != (a * per + core) * split + r))
                def _():
                    start = s * size + r * piece
                    await_bytes(result.at[a, start : start + piece, :], fin_recv.at[s, a, r])

    out_ref[...] = result[0]
    grad_ref[...] = result[1]


def body(tokens, cotangent, gate_weight, up_weight, down_weight, gate_mask, up_mask, down_mask):
    rows, cols = lax.axis_size("row"), lax.axis_size("col")
    per = cols // rows
    local_tokens, feats = tokens.shape
    depth, hidden = gate_weight.shape
    size = min(TOKEN_BLOCK, local_tokens)
    width = min(WIDTH, hidden)
    slices = hidden // width
    subs = local_tokens // size
    blocks = rows * subs
    chunks = blocks * slices
    split = max(1, min(cols // (2 * per), size // 16))
    reducers = 2 * per * split
    piece = size // split
    dma = pltpu.SemaphoreType.DMA
    vmem = pl.BlockSpec(memory_space=pltpu.VMEM)
    smem = pl.BlockSpec(memory_space=pltpu.SMEM)
    hbm = pl.BlockSpec(memory_space=pl.ANY)
    shard = jax.ShapeDtypeStruct((local_tokens, feats), bf16)
    return pl.pallas_call(
        functools.partial(layer_kernel, rows, cols),
        out_shape=(shard, shard),
        in_specs=[vmem, vmem, hbm, hbm, hbm, smem, smem, smem],
        out_specs=(vmem, vmem),
        scratch_shapes=[
            pltpu.VMEM((slices, depth, width), bf16),
            pltpu.VMEM((slices, depth, width), bf16),
            pltpu.VMEM((slices, width, depth), bf16),
            pltpu.VMEM((blocks, per, 2, size, feats), bf16),
            pltpu.VMEM((chunks, 3, size, width), f32),
            pltpu.VMEM((2, chunks, 3, size, width), bf16),
            pltpu.VMEM((2, size, depth), f32),
            pltpu.VMEM((blocks, reducers, piece, feats), bf16),
            pltpu.VMEM((blocks, cols - 1, piece, feats), bf16),
            pltpu.VMEM((blocks, piece, feats), bf16),
            pltpu.VMEM((2, local_tokens, feats), bf16),
            dma((3, slices)),
            dma((2, chunks)),
            dma((2, chunks)),
            dma((subs, 2)),
            dma((blocks, per)),
            dma((blocks, rows - 1)),
            dma((blocks, per - 1)),
            dma((blocks, cols - 1)),
            dma((blocks,)),
            dma((blocks,)),
            dma((subs, 2, split)),
        ],
        compiler_params=pltpu.CompilerParams(
            collective_id=0, has_side_effects=True, vmem_limit_bytes=58 * 1024 * 1024
        ),
        name="layer",
    )(tokens, cotangent, gate_weight, up_weight, down_weight, gate_mask, up_mask, down_mask)


def solution(mesh):
    in_specs = (
        P("row", "col"),
        P("row", "col"),
        P("row", "col"),
        P("row", "col"),
        P("col", "row"),
        P("row", "col"),
        P("row", "col"),
        P("col", "row"),
    )
    out_specs = (P("row", "col"), P("row", "col"))
    return jax.shard_map(body, mesh=mesh, in_specs=in_specs, out_specs=out_specs, check_vma=False)
```

```python
import functools

import jax
import jax.numpy as jnp
from jax import lax
from jax.experimental import pallas as pl
from jax.experimental.pallas import tpu as pltpu
from jax.sharding import PartitionSpec as P

BLOCK = 128
TOKEN_BLOCK = 64
WIDTH = 256
LAG = 3
CONTRACT = (((1,), (1,)), ((), ()))
MESH_ID = pl.DeviceIdType.MESH
bf16, f32 = jnp.bfloat16, jnp.float32


def remote(src, dst, send, recv, row, col):
    return pltpu.make_async_remote_copy(
        src_ref=src, dst_ref=dst, send_sem=send, recv_sem=recv,
        device_id={"row": row, "col": col}, device_id_type=MESH_ID,
    )


def await_bytes(ref, sem):
    pltpu.make_async_copy(ref, ref, sem).wait()


def layer_kernel(
    rows, cols, tok_ref, cot_ref, wg_hbm, wu_hbm, wd_hbm, gm_ref, um_ref, dm_ref, out_ref,
    wg, wu, wd, panel, stage, own, sums, acc, pout, land, total, result,
    w_sem, ch_send, ch_recv, src_send, stage_recv, col_send, col_recv, gather_send, pan_recv, rs_send, rs_recv, fin_send, fin_recv,
):
    row, col = lax.axis_index("row"), lax.axis_index("col")
    last = rows - 1
    per = cols // rows
    chip, core = col // per, col % per
    blocks, _, _, size, feats = panel.shape
    slices, _, width = wg.shape
    subs = blocks // rows
    chunks = blocks * slices
    _, reducers, piece, _ = pout.shape
    split = reducers // (2 * per)
    slab = stage.shape[3]
    relays = size // slab

    low = row < rows // 2
    near, far = jnp.where(low, 0, 1), jnp.where(low, 1, 0)
    near_pos, far_pos = jnp.minimum(row, last - row), jnp.maximum(row, last - row)
    near_next = jnp.where(low, row + 1, row - 1)
    far_next = jnp.clip(jnp.where(low, row - 1, row + 1), 0, last)

    def load(j):
        span = pl.ds(pl.multiple_of(j * width, width), width)
        return (
            pltpu.make_async_copy(wg_hbm.at[:, span], wg.at[j], w_sem.at[0, j]),
            pltpu.make_async_copy(wu_hbm.at[:, span], wu.at[j], w_sem.at[1, j]),
            pltpu.make_async_copy(wd_hbm.at[span, :], wd.at[j], w_sem.at[2, j]),
        )

    def load_start(j, carry):
        for copy in load(j):
            copy.start()
        return carry

    lax.fori_loop(0, slices, load_start, 0)

    barrier = pltpu.get_barrier_semaphore()

    def greet(i, carry):
        @pl.when(i != row * cols + col)
        def _():
            pl.semaphore_signal(
                barrier, inc=1, device_id={"row": i // cols, "col": i % cols}, device_id_type=MESH_ID
            )
        return carry

    lax.fori_loop(0, rows * cols, greet, 0)
    pl.semaphore_wait(barrier, rows * cols - 1)

    def prune(j):
        for copy in load(j):
            copy.wait()
        for i in range(wg.shape[1] // BLOCK):
            for n in range(width // BLOCK):
                at = j * (width // BLOCK) + n
                feat, hid = slice(i * BLOCK, (i + 1) * BLOCK), slice(n * BLOCK, (n + 1) * BLOCK)
                wg[j, feat, hid] = wg[j, feat, hid] * jnp.full((BLOCK, BLOCK), gm_ref[i, at].astype(f32)).astype(bf16)
                wu[j, feat, hid] = wu[j, feat, hid] * jnp.full((BLOCK, BLOCK), um_ref[i, at].astype(f32)).astype(bf16)
                wd[j, hid, feat] = wd[j, hid, feat] * jnp.full((BLOCK, BLOCK), dm_ref[i, at].astype(f32)).astype(bf16)

    def rows_of(t, g):
        return pl.ds(pl.multiple_of((t % subs) * size + g * slab, slab), slab)

    def source_copies(t, off):
        g = lax.rem(chip + off, rows)
        return [
            remote(
                ref.at[rows_of(t, g % relays), :], stage.at[t % subs, chip, i], src_send.at[t % subs, off - 1, i],
                stage_recv.at[t % subs, chip], row, g * per + core,
            )
            for i, ref in enumerate((tok_ref, cot_ref))
        ]

    def source(t):
        @pl.when(row == t // subs)
        def _():
            for off in range(1, rows):
                @pl.when(lax.rem(chip + off, rows) < relays)
                def _():
                    for copy in source_copies(t, off):
                        copy.start()

            @pl.when(chip < relays)
            def _():
                stage[t % subs, chip, 0] = tok_ref[rows_of(t, chip % relays), :]
                stage[t % subs, chip, 1] = cot_ref[rows_of(t, chip % relays), :]

    mine = pl.ds(pl.multiple_of((chip % relays) * slab, slab), slab)

    def column_copy(t, a):
        return remote(
            stage.at[t % subs, a], panel.at[t, core, :, mine, :], col_send.at[t % subs, a], col_recv.at[t], a, col
        )

    def relay(t):
        @pl.when((row == t // subs) & (chip < relays))
        def _():
            for off in range(1, rows):
                a = lax.rem(row + off, rows)

                @pl.when(a != chip)
                def _():
                    await_bytes(stage.at[t % subs, a], stage_recv.at[t % subs, a])

                column_copy(t, a).start()

            @pl.when(row != chip)
            def _():
                await_bytes(stage.at[t % subs, row], stage_recv.at[t % subs, row])

            panel[t, core, :, mine, :] = stage[t % subs, row]

    def gather_copy(t, off):
        return remote(
            panel.at[t, core, :, mine, :], panel.at[t, core, :, mine, :], gather_send.at[t, off - 1],
            pan_recv.at[t, core, chip % relays], row, lax.rem(col + off, cols),
        )

    def gather(t):
        @pl.when(chip < relays)
        def _():
            @pl.when(row != t // subs)
            def _():
                await_bytes(panel.at[t, core, :, mine, :], col_recv.at[t])

            for off in range(1, cols):
                gather_copy(t, off).start()

    def arrive(t):
        for h in range(per):
            for g in range(relays):
                @pl.when((core != h) | (chip != g))
                def _():
                    await_bytes(panel.at[t, h, :, g * slab : (g + 1) * slab, :], pan_recv.at[t, h, g])

    def near_copy(k):
        return remote(
            sums.at[near, k], sums.at[near, k], ch_send.at[near, k], ch_recv.at[near, k], near_next, col
        )

    def far_copy(k):
        return remote(sums.at[far, k], sums.at[far, k], ch_send.at[far, k], ch_recv.at[far, k], far_next, col)

    def project(k):
        t, j = k // slices, k % slices

        @pl.when(k < slices)
        def _():
            prune(k)

        @pl.when(j == 0)
        def _():
            arrive(t)

        gate = up = grad = 0.0
        for h in range(per):
            feat = slice(h * feats, (h + 1) * feats)
            tok, cot = panel[t, h, 0], panel[t, h, 1]
            gate += jnp.dot(tok, wg[j, feat, :], preferred_element_type=f32)
            up += jnp.dot(tok, wu[j, feat, :], preferred_element_type=f32)
            grad += lax.dot_general(cot, wd[j, :, feat], CONTRACT, preferred_element_type=f32)
        own[k, 0] = gate
        own[k, 1] = up
        own[k, 2] = grad

    def pass_near(k):
        @pl.when(near_pos == 0)
        def _():
            sums[near, k] = own[k].astype(bf16)

        @pl.when(near_pos > 0)
        def _():
            near_copy(k).wait_recv()
            sums[near, k] = (own[k] + sums[near, k].astype(f32)).astype(bf16)

        near_copy(k).start()

    def pass_far(k):
        t, j = k // slices, k % slices
        far_copy(k).wait_recv()
        came = sums[far, k].astype(f32)
        whole = came + sums[near, k].astype(f32)

        @pl.when(far_pos < last)
        def _():
            sums[far, k] = (own[k] + came).astype(bf16)
            far_copy(k).start()

        gate, up, grad = whole[0], whole[1], whole[2]
        sigma = jax.nn.sigmoid(gate)
        silu = gate * sigma
        hidden = (silu * up).astype(bf16)
        grad_gate = (grad * up * sigma * (1.0 + gate * (1.0 - sigma))).astype(bf16)
        grad_up = (grad * silu).astype(bf16)

        @pl.when(j == 0)
        def _():
            acc[...] = jnp.zeros_like(acc)

        acc[0] += jnp.dot(hidden, wd[j], preferred_element_type=f32)
        acc[1] += lax.dot_general(grad_gate, wg[j], CONTRACT, preferred_element_type=f32) + lax.dot_general(
            grad_up, wu[j], CONTRACT, preferred_element_type=f32
        )

        @pl.when((j == slices // 2) & (t > 0))
        def _():
            combine(t - 1)

        @pl.when(j == slices - 1)
        def _():
            scatter(t)

    def scatter_copy(t, off):
        return remote(
            pout.at[t, lax.rem(col + off, cols) % reducers], land.at[t, cols - 1 - off], rs_send.at[t, off - 1],
            rs_recv.at[t], row, lax.rem(col + off, cols),
        )

    def scatter(t):
        for a in range(2):
            for h in range(per):
                for r in range(split):
                    pout[t, (a * per + h) * split + r] = acc[
                        a, r * piece : (r + 1) * piece, h * feats : (h + 1) * feats
                    ].astype(bf16)
        for off in range(1, cols):
            @pl.when(lax.rem(col + off, cols) < reducers)
            def _():
                scatter_copy(t, off).start()

    part = col % split
    half = (col // split) % per
    which = lax.rem(col // (split * per), 2)
    owner_col = row * per + half

    def give(t):
        span = pl.ds(pl.multiple_of((t % subs) * size + part * piece, piece), piece)
        return remote(
            total.at[t], result.at[which, span, :], fin_send.at[t], fin_recv.at[t % subs, which, part],
            t // subs, owner_col,
        )

    def combine(t):
        @pl.when(col < reducers)
        def _():
            await_bytes(land.at[t], rs_recv.at[t])
            value = pout[t, col % reducers].astype(f32)
            for i in range(cols - 1):
                value = value + land[t, i].astype(f32)
            mine = (row == t // subs) & (col == owner_col)

            @pl.when(mine)
            def _():
                span = pl.ds(pl.multiple_of((t % subs) * size + part * piece, piece), piece)
                result[which, span, :] = value.astype(bf16)

            @pl.when(jnp.logical_not(mine))
            def _():
                total[t] = value.astype(bf16)
                give(t).start()

    source(0)
    if blocks > 1:
        source(1)
    relay(0)
    gather(0)
    project(0)

    def step(s, carry):
        t, j = s // slices, s % slices

        if blocks > 1:
            @pl.when(s == 0)
            def _():
                relay(1)

            @pl.when(s == 1)
            def _():
                gather(1)

        @pl.when((j == 0) & (t + 2 < blocks))
        def _():
            source(t + 2)

        @pl.when((j == slices // 4) & (t + 2 < blocks))
        def _():
            relay(t + 2)

        @pl.when((j == slices * 5 // 8) & (t + 2 < blocks))
        def _():
            gather(t + 2)

        k_near = s - LAG * near_pos
        k_far = s - LAG * far_pos

        @pl.when((k_near >= 0) & (k_near < chunks))
        def _():
            pass_near(k_near)

        @pl.when((k_far >= 0) & (k_far < chunks))
        def _():
            pass_far(k_far)

        @pl.when(s + 1 < chunks)
        def _():
            project(s + 1)

        return carry

    lax.fori_loop(0, chunks + LAG * last, step, 0)
    combine(blocks - 1)

    def drain_chunk(k, carry):
        near_copy(k).wait_send()

        @pl.when(far_pos < last)
        def _():
            far_copy(k).wait_send()

        return carry

    lax.fori_loop(0, chunks, drain_chunk, 0)

    def drain_block(t, carry):
        @pl.when(row == t // subs)
        def _():
            for off in range(1, rows):
                @pl.when(lax.rem(chip + off, rows) < relays)
                def _():
                    for copy in source_copies(t, off):
                        copy.wait_send()

        @pl.when((row == t // subs) & (chip < relays))
        def _():
            for off in range(1, rows):
                column_copy(t, lax.rem(row + off, rows)).wait_send()

        @pl.when(chip < relays)
        def _():
            for off in range(1, cols):
                gather_copy(t, off).wait_send()

        for off in range(1, cols):
            @pl.when(lax.rem(col + off, cols) < reducers)
            def _():
                scatter_copy(t, off).wait_send()

        @pl.when((col < reducers) & jnp.logical_not((row == t // subs) & (col == owner_col)))
        def _():
            give(t).wait_send()

        return carry

    lax.fori_loop(0, blocks, drain_block, 0)

    for s in range(subs):
        for a in range(2):
            for r in range(split):
                @pl.when((row != chip) | (col != (a * per + core) * split + r))
                def _():
                    start = s * size + r * piece
                    await_bytes(result.at[a, start : start + piece, :], fin_recv.at[s, a, r])

    out_ref[...] = result[...]


def unstack_kernel(pair_ref, out_ref, grad_ref):
    out_ref[...] = pair_ref[0]
    grad_ref[...] = pair_ref[1]


def body(tokens, cotangent, gate_weight, up_weight, down_weight, gate_mask, up_mask, down_mask):
    rows, cols = lax.axis_size("row"), lax.axis_size("col")
    per = cols // rows
    local_tokens, feats = tokens.shape
    depth, hidden = gate_weight.shape
    size = min(TOKEN_BLOCK, local_tokens)
    width = min(WIDTH, hidden)
    slices = hidden // width
    subs = local_tokens // size
    blocks = rows * subs
    chunks = blocks * slices
    split = max(1, min(cols // (2 * per), size // 16))
    reducers = 2 * per * split
    piece = size // split
    relays = max(1, min(rows, size // 16))
    dma = pltpu.SemaphoreType.DMA
    vmem = pl.BlockSpec(memory_space=pltpu.VMEM)
    smem = pl.BlockSpec(memory_space=pltpu.SMEM)
    hbm = pl.BlockSpec(memory_space=pl.ANY)
    shard = jax.ShapeDtypeStruct((local_tokens, feats), bf16)
    pair = pl.pallas_call(
        functools.partial(layer_kernel, rows, cols),
        out_shape=jax.ShapeDtypeStruct((2, local_tokens, feats), bf16),
        in_specs=[vmem, vmem, hbm, hbm, hbm, smem, smem, smem],
        out_specs=vmem,
        scratch_shapes=[
            pltpu.VMEM((slices, depth, width), bf16),
            pltpu.VMEM((slices, depth, width), bf16),
            pltpu.VMEM((slices, width, depth), bf16),
            pltpu.VMEM((blocks, per, 2, size, feats), bf16),
            pltpu.VMEM((subs, rows, 2, size // relays, feats), bf16),
            pltpu.VMEM((chunks, 3, size, width), f32),
            pltpu.VMEM((2, chunks, 3, size, width), bf16),
            pltpu.VMEM((2, size, depth), f32),
            pltpu.VMEM((blocks, reducers, piece, feats), bf16),
            pltpu.VMEM((blocks, cols - 1, piece, feats), bf16),
            pltpu.VMEM((blocks, piece, feats), bf16),
            pltpu.VMEM((2, local_tokens, feats), bf16),
            dma((3, slices)),
            dma((2, chunks)),
            dma((2, chunks)),
            dma((subs, rows - 1, 2)),
            dma((subs, rows)),
            dma((subs, rows)),
            dma((blocks,)),
            dma((blocks, cols - 1)),
            dma((blocks, per, relays)),
            dma((blocks, cols - 1)),
            dma((blocks,)),
            dma((blocks,)),
            dma((subs, 2, split)),
        ],
        compiler_params=pltpu.CompilerParams(
            collective_id=0, has_side_effects=True, vmem_limit_bytes=58 * 1024 * 1024
        ),
        name="layer",
    )(tokens, cotangent, gate_weight, up_weight, down_weight, gate_mask, up_mask, down_mask.T)
    return pl.pallas_call(
        unstack_kernel, out_shape=(shard, shard), in_specs=[vmem], out_specs=(vmem, vmem), name="unstack"
    )(pair)


def solution(mesh):
    in_specs = (
        P("row", "col"),
        P("row", "col"),
        P("row", "col"),
        P("row", "col"),
        P("col", "row"),
        P("row", "col"),
        P("row", "col"),
        P("col", "row"),
    )
    out_specs = (P("row", "col"), P("row", "col"))
    return jax.shard_map(body, mesh=mesh, in_specs=in_specs, out_specs=out_specs, check_vma=False)
```

```python
import functools

import jax
import jax.numpy as jnp
from jax import lax
from jax.experimental import pallas as pl
from jax.experimental.pallas import tpu as pltpu
from jax.sharding import PartitionSpec as P

BLOCK = 128
TOKEN_BLOCK = 64
WIDTH = 256
LAG = 3
FIRST_LAG = 2
WIDEN = 16
PARTED = 2
EARLY = 3
GATHER_AT = 3
DEFER = 3
CONTRACT = (((1,), (1,)), ((), ()))
MESH_ID = pl.DeviceIdType.MESH
bf16, f32 = jnp.bfloat16, jnp.float32


def remote(src, dst, send, recv, row, col):
    return pltpu.make_async_remote_copy(
        src_ref=src, dst_ref=dst, send_sem=send, recv_sem=recv,
        device_id={"row": row, "col": col}, device_id_type=MESH_ID,
    )


def await_bytes(ref, sem):
    pltpu.make_async_copy(ref, ref, sem).wait()


def layer_kernel(
    rows, cols, tok_ref, cot_ref, wg_hbm, wu_hbm, wd_hbm, gm_ref, um_ref, dm_ref, out_ref,
    wg, wu, wd, panel, stage, own, sums, both, acc, pout, land, total, result,
    w_sem, ch_send, ch_recv, part_send, part_recv, src_send, stage_recv, col_send, col_recv, gather_send, pan_recv, rs_send, rs_recv, fin_send, fin_recv,
):
    row, col = lax.axis_index("row"), lax.axis_index("col")
    last = rows - 1
    per = cols // rows
    chip, core = col // per, col % per
    blocks, _, _, size, feats = panel.shape
    slices, _, width = wg.shape
    subs = blocks // rows
    chunks = blocks * slices
    _, reducers, piece, _ = pout.shape
    split = reducers // (2 * per)
    slab = stage.shape[3]
    relays = size // slab
    parted = part_send.shape[1]

    low = row < rows // 2
    near, far = jnp.where(low, 0, 1), jnp.where(low, 1, 0)
    near_pos, far_pos = jnp.minimum(row, last - row), jnp.maximum(row, last - row)
    near_next = jnp.where(low, row + 1, row - 1)
    far_next = jnp.clip(jnp.where(low, row - 1, row + 1), 0, last)

    def load(j):
        span = pl.ds(pl.multiple_of(j * width, width), width)
        return (
            pltpu.make_async_copy(wg_hbm.at[:, span], wg.at[j], w_sem.at[0, j]),
            pltpu.make_async_copy(wu_hbm.at[:, span], wu.at[j], w_sem.at[1, j]),
            pltpu.make_async_copy(wd_hbm.at[span, :], wd.at[j], w_sem.at[2, j]),
        )

    def load_start(j, carry):
        for copy in load(j):
            copy.start()
        return carry

    lax.fori_loop(0, slices, load_start, 0)

    barrier = pltpu.get_barrier_semaphore()

    def greet(i, carry):
        @pl.when(i != row * cols + col)
        def _():
            pl.semaphore_signal(
                barrier, inc=1, device_id={"row": i // cols, "col": i % cols}, device_id_type=MESH_ID
            )
        return carry

    lax.fori_loop(0, rows * cols, greet, 0)
    pl.semaphore_wait(barrier, rows * cols - 1)

    def prune(j):
        for copy in load(j):
            copy.wait()
        for i in range(wg.shape[1] // BLOCK):
            for n in range(width // BLOCK):
                at = j * (width // BLOCK) + n
                feat, hid = slice(i * BLOCK, (i + 1) * BLOCK), slice(n * BLOCK, (n + 1) * BLOCK)
                wg[j, feat, hid] = wg[j, feat, hid] * jnp.full((BLOCK, BLOCK), gm_ref[i, at].astype(f32)).astype(bf16)
                wu[j, feat, hid] = wu[j, feat, hid] * jnp.full((BLOCK, BLOCK), um_ref[i, at].astype(f32)).astype(bf16)
                wd[j, hid, feat] = wd[j, hid, feat] * jnp.full((BLOCK, BLOCK), dm_ref[i, at].astype(f32)).astype(bf16)

    def rows_of(t, g):
        return pl.ds(pl.multiple_of((t % subs) * size + g * slab, slab), slab)

    def source_copies(t, off):
        g = lax.rem(chip + off, rows)
        return [
            remote(
                ref.at[rows_of(t, g % relays), :], stage.at[t % subs, chip, i], src_send.at[t % subs, off - 1, i],
                stage_recv.at[t % subs, chip], row, g * per + core,
            )
            for i, ref in enumerate((tok_ref, cot_ref))
        ]

    def source(t):
        @pl.when(row == t // subs)
        def _():
            for off in range(1, rows):
                @pl.when(lax.rem(chip + off, rows) < relays)
                def _():
                    for copy in source_copies(t, off):
                        copy.start()

            @pl.when(chip < relays)
            def _():
                stage[t % subs, chip, 0] = tok_ref[rows_of(t, chip % relays), :]
                stage[t % subs, chip, 1] = cot_ref[rows_of(t, chip % relays), :]

    mine = pl.ds(pl.multiple_of((chip % relays) * slab, slab), slab)

    def column_copy(t, a):
        return remote(
            stage.at[t % subs, a], panel.at[t, core, :, mine, :], col_send.at[t % subs, a], col_recv.at[t], a, col
        )

    def relay(t):
        @pl.when((row == t // subs) & (chip < relays))
        def _():
            for off in range(1, rows):
                a = lax.rem(row + off, rows)

                @pl.when(a != chip)
                def _():
                    await_bytes(stage.at[t % subs, a], stage_recv.at[t % subs, a])

                column_copy(t, a).start()

            @pl.when(row != chip)
            def _():
                await_bytes(stage.at[t % subs, row], stage_recv.at[t % subs, row])

            panel[t, core, :, mine, :] = stage[t % subs, row]

    def gather_copy(t, off):
        return remote(
            panel.at[t, core, :, mine, :], panel.at[t, core, :, mine, :], gather_send.at[t, off - 1],
            pan_recv.at[t, core, chip % relays], row, lax.rem(col + off, cols),
        )

    def gather(t):
        @pl.when(chip < relays)
        def _():
            @pl.when(row != t // subs)
            def _():
                await_bytes(panel.at[t, core, :, mine, :], col_recv.at[t])

            for off in range(1, cols):
                gather_copy(t, off).start()

    def arrive(t):
        for h in range(per):
            for g in range(relays):
                @pl.when((core != h) | (chip != g))
                def _():
                    await_bytes(panel.at[t, h, :, g * slab : (g + 1) * slab, :], pan_recv.at[t, h, g])

    def near_copy(k):
        return remote(
            sums.at[near, k], sums.at[near, k], ch_send.at[near, k], ch_recv.at[near, k], near_next, col
        )

    def far_copy(k):
        return remote(sums.at[far, k], sums.at[far, k], ch_send.at[far, k], ch_recv.at[far, k], far_next, col)

    def near_part(k, i):
        k = k % parted
        return remote(
            sums.at[near, k, i], sums.at[near, k, i], part_send.at[near, k, i], part_recv.at[near, k, i], near_next, col
        )

    def far_part(k, i):
        k = k % parted
        return remote(
            sums.at[far, k, i], sums.at[far, k, i], part_send.at[far, k, i], part_recv.at[far, k, i], far_next, col
        )

    def project(k):
        t, j = k // slices, k % slices

        @pl.when((k >= min(EARLY, slices)) & (k < slices))
        def _():
            prune(k)

        @pl.when(j == 0)
        def _():
            arrive(t)

        gate = up = grad = 0.0
        for h in range(per):
            feat = slice(h * feats, (h + 1) * feats)
            tok, cot = panel[t, h, 0], panel[t, h, 1]
            gate += jnp.dot(tok, wg[j, feat, :], preferred_element_type=f32)
            up += jnp.dot(tok, wu[j, feat, :], preferred_element_type=f32)
            grad += lax.dot_general(cot, wd[j, :, feat], CONTRACT, preferred_element_type=f32)
        own[k, 0] = gate
        own[k, 1] = up
        own[k, 2] = grad

    def pass_near(k):
        @pl.when(k < parted)
        def _():
            for i in range(3):
                @pl.when(near_pos == 0)
                def _():
                    sums[near, k, i] = own[k, i].astype(bf16)

                @pl.when(near_pos > 0)
                def _():
                    near_part(k, i).wait_recv()
                    sums[near, k, i] = (own[k, i] + sums[near, k, i].astype(f32)).astype(bf16)

                near_part(k, i).start()

        @pl.when(k >= parted)
        def _():
            @pl.when(near_pos == 0)
            def _():
                sums[near, k] = own[k].astype(bf16)

            @pl.when(near_pos > 0)
            def _():
                near_copy(k).wait_recv()
                sums[near, k] = (own[k] + sums[near, k].astype(f32)).astype(bf16)

            near_copy(k).start()

    def pass_far(k):
        t, j = k // slices, k % slices

        @pl.when(k < parted)
        def _():
            for i in range(3):
                far_part(k, i).wait_recv()
                came = sums[far, k, i].astype(f32)
                both[i] = came + sums[near, k, i].astype(f32)

                @pl.when(far_pos < last)
                def _():
                    sums[far, k, i] = (own[k, i] + came).astype(bf16)
                    far_part(k, i).start()

        @pl.when(k >= parted)
        def _():
            far_copy(k).wait_recv()
            came = sums[far, k].astype(f32)
            both[...] = came + sums[near, k].astype(f32)

            @pl.when(far_pos < last)
            def _():
                sums[far, k] = (own[k] + came).astype(bf16)
                far_copy(k).start()

        gate, up, grad = both[0], both[1], both[2]
        sigma = jax.nn.sigmoid(gate)
        silu = gate * sigma
        hidden = (silu * up).astype(bf16)
        grad_gate = (grad * up * sigma * (1.0 + gate * (1.0 - sigma))).astype(bf16)
        grad_up = (grad * silu).astype(bf16)

        @pl.when(j == 0)
        def _():
            acc[...] = jnp.zeros_like(acc)

        acc[0] += jnp.dot(hidden, wd[j], preferred_element_type=f32)
        acc[1] += lax.dot_general(grad_gate, wg[j], CONTRACT, preferred_element_type=f32) + lax.dot_general(
            grad_up, wu[j], CONTRACT, preferred_element_type=f32
        )

        @pl.when((j == slices // 2) & (t > 0))
        def _():
            combine(t - 1)

        @pl.when(j == slices - 1)
        def _():
            scatter(t)

    def scatter_copy(t, off):
        return remote(
            pout.at[t, lax.rem(col + off, cols) % reducers], land.at[t, cols - 1 - off], rs_send.at[t, off - 1],
            rs_recv.at[t], row, lax.rem(col + off, cols),
        )

    def scatter(t):
        for a in range(2):
            for h in range(per):
                for r in range(split):
                    pout[t, (a * per + h) * split + r] = acc[
                        a, r * piece : (r + 1) * piece, h * feats : (h + 1) * feats
                    ].astype(bf16)
        for off in range(1, cols):
            @pl.when(lax.rem(col + off, cols) < reducers)
            def _():
                scatter_copy(t, off).start()

    part = col % split
    half = (col // split) % per
    which = lax.rem(col // (split * per), 2)
    owner_col = row * per + half

    def give(t):
        span = pl.ds(pl.multiple_of((t % subs) * size + part * piece, piece), piece)
        return remote(
            total.at[t], result.at[which, span, :], fin_send.at[t], fin_recv.at[t % subs, which, part],
            t // subs, owner_col,
        )

    def combine(t):
        @pl.when(col < reducers)
        def _():
            await_bytes(land.at[t], rs_recv.at[t])
            value = pout[t, col % reducers].astype(f32)
            for i in range(cols - 1):
                value = value + land[t, i].astype(f32)
            mine = (row == t // subs) & (col == owner_col)

            @pl.when(mine)
            def _():
                span = pl.ds(pl.multiple_of((t % subs) * size + part * piece, piece), piece)
                result[which, span, :] = value.astype(bf16)

            @pl.when(jnp.logical_not(mine))
            def _():
                total[t] = value.astype(bf16)

                @pl.when((t < blocks - 1 - DEFER) | (t == blocks - 1))
                def _():
                    give(t).start()

    source(row * subs)

    @pl.when(row != 0)
    def _():
        for u in range(1, subs):
            source(row * subs + u)

    relay(0)
    gather(0)

    @pl.when(row == 0)
    def _():
        for u in range(1, subs):
            source(u)

    @pl.when(row != 0)
    def _():
        relay(row * subs)

    for u in range(1, subs):
        relay(row * subs + u)

    for j in range(min(EARLY, slices)):
        prune(j)
    project(0)

    def turn(s, pos):
        def at(s):
            return s - FIRST_LAG * pos - jnp.clip(s - WIDEN, 0, (LAG - FIRST_LAG) * pos)

        k = at(s)
        return k, (k >= 0) & (k < chunks) & (k != at(s - 1))

    def step(s, carry):
        t, j = s // slices, s % slices

        @pl.when((j == GATHER_AT * slices // 8) & (t + 1 < blocks))
        def _():
            gather(t + 1)

        k_near, do_near = turn(s, near_pos)
        k_far, do_far = turn(s, far_pos)

        @pl.when(do_near)
        def _():
            pass_near(k_near)

        @pl.when(do_far)
        def _():
            pass_far(k_far)

        @pl.when(s + 1 < chunks)
        def _():
            project(s + 1)

        return carry

    lax.fori_loop(0, chunks + LAG * last, step, 0)
    def give_late(t, carry):
        @pl.when((col < reducers) & jnp.logical_not((row == t // subs) & (col == owner_col)))
        def _():
            give(t).start()

        return carry

    lax.fori_loop(max(0, blocks - 1 - DEFER), blocks - 1, give_late, 0)

    for k in range(parted):
        for i in range(3):
            near_part(k, i).wait_send()

            @pl.when(far_pos < last)
            def _():
                far_part(k, i).wait_send()

    def drain_chunk(k, carry):
        near_copy(k).wait_send()

        @pl.when(far_pos < last)
        def _():
            far_copy(k).wait_send()

        return carry

    lax.fori_loop(parted, chunks, drain_chunk, 0)

    def drain_block(t, carry):
        @pl.when(row == t // subs)
        def _():
            for off in range(1, rows):
                @pl.when(lax.rem(chip + off, rows) < relays)
                def _():
                    for copy in source_copies(t, off):
                        copy.wait_send()

        @pl.when((row == t // subs) & (chip < relays))
        def _():
            for off in range(1, rows):
                column_copy(t, lax.rem(row + off, rows)).wait_send()

        @pl.when(chip < relays)
        def _():
            for off in range(1, cols):
                gather_copy(t, off).wait_send()

        return carry

    lax.fori_loop(0, blocks, drain_block, 0)
    combine(blocks - 1)

    def drain_collect(t, carry):
        for off in range(1, cols):
            @pl.when(lax.rem(col + off, cols) < reducers)
            def _():
                scatter_copy(t, off).wait_send()

        @pl.when((col < reducers) & jnp.logical_not((row == t // subs) & (col == owner_col)))
        def _():
            give(t).wait_send()

        return carry

    lax.fori_loop(0, blocks, drain_collect, 0)

    for s in range(subs):
        for a in range(2):
            for r in range(split):
                @pl.when((row != chip) | (col != (a * per + core) * split + r))
                def _():
                    start = s * size + r * piece
                    await_bytes(result.at[a, start : start + piece, :], fin_recv.at[s, a, r])

    out_ref[...] = result[...]


def unstack_kernel(pair_ref, out_ref, grad_ref):
    out_ref[...] = pair_ref[0]
    grad_ref[...] = pair_ref[1]


def body(tokens, cotangent, gate_weight, up_weight, down_weight, gate_mask, up_mask, down_mask):
    rows, cols = lax.axis_size("row"), lax.axis_size("col")
    per = cols // rows
    local_tokens, feats = tokens.shape
    depth, hidden = gate_weight.shape
    size = min(TOKEN_BLOCK, local_tokens)
    width = min(WIDTH, hidden)
    slices = hidden // width
    subs = local_tokens // size
    blocks = rows * subs
    chunks = blocks * slices
    split = max(1, min(cols // (2 * per), size // 16))
    reducers = 2 * per * split
    piece = size // split
    relays = max(1, min(rows, size // 16))
    dma = pltpu.SemaphoreType.DMA
    vmem = pl.BlockSpec(memory_space=pltpu.VMEM)
    smem = pl.BlockSpec(memory_space=pltpu.SMEM)
    hbm = pl.BlockSpec(memory_space=pl.ANY)
    shard = jax.ShapeDtypeStruct((local_tokens, feats), bf16)
    pair = pl.pallas_call(
        functools.partial(layer_kernel, rows, cols),
        out_shape=jax.ShapeDtypeStruct((2, local_tokens, feats), bf16),
        in_specs=[vmem, vmem, hbm, hbm, hbm, smem, smem, smem],
        out_specs=vmem,
        scratch_shapes=[
            pltpu.VMEM((slices, depth, width), bf16),
            pltpu.VMEM((slices, depth, width), bf16),
            pltpu.VMEM((slices, width, depth), bf16),
            pltpu.VMEM((blocks, per, 2, size, feats), bf16),
            pltpu.VMEM((subs, rows, 2, size // relays, feats), bf16),
            pltpu.VMEM((chunks, 3, size, width), f32),
            pltpu.VMEM((2, chunks, 3, size, width), bf16),
            pltpu.VMEM((3, size, width), f32),
            pltpu.VMEM((2, size, depth), f32),
            pltpu.VMEM((blocks, reducers, piece, feats), bf16),
            pltpu.VMEM((blocks, cols - 1, piece, feats), bf16),
            pltpu.VMEM((blocks, piece, feats), bf16),
            pltpu.VMEM((2, local_tokens, feats), bf16),
            dma((3, slices)),
            dma((2, chunks)),
            dma((2, chunks)),
            dma((2, min(PARTED, chunks), 3)),
            dma((2, min(PARTED, chunks), 3)),
            dma((subs, rows - 1, 2)),
            dma((subs, rows)),
            dma((subs, rows)),
            dma((blocks,)),
            dma((blocks, cols - 1)),
            dma((blocks, per, relays)),
            dma((blocks, cols - 1)),
            dma((blocks,)),
            dma((blocks,)),
            dma((subs, 2, split)),
        ],
        compiler_params=pltpu.CompilerParams(
            collective_id=0, has_side_effects=True, vmem_limit_bytes=58 * 1024 * 1024
        ),
        name="layer",
    )(tokens, cotangent, gate_weight, up_weight, down_weight, gate_mask, up_mask, down_mask.T)
    return pl.pallas_call(
        unstack_kernel, out_shape=(shard, shard), in_specs=[vmem], out_specs=(vmem, vmem), name="unstack"
    )(pair)


def solution(mesh):
    in_specs = (
        P("row", "col"),
        P("row", "col"),
        P("row", "col"),
        P("row", "col"),
        P("col", "row"),
        P("row", "col"),
        P("row", "col"),
        P("col", "row"),
    )
    out_specs = (P("row", "col"), P("row", "col"))
    return jax.shard_map(body, mesh=mesh, in_specs=in_specs, out_specs=out_specs, check_vma=False)
```

```python
import functools

import jax
import jax.numpy as jnp
from jax import lax
from jax.experimental import pallas as pl
from jax.experimental.pallas import tpu as pltpu
from jax.sharding import PartitionSpec as P

BLOCK = 128
TOKEN_BLOCK = 64
WIDTH = 256
LAG = 3
HEAD = 0
TAIL = 0
ORDER = 1
PARTED = 2
EARLY = 3
GATHER_AT = 3
DEFER = 3
CONTRACT = (((1,), (1,)), ((), ()))
MESH_ID = pl.DeviceIdType.MESH
bf16, f32 = jnp.bfloat16, jnp.float32


def remote(src, dst, send, recv, row, col):
    return pltpu.make_async_remote_copy(
        src_ref=src, dst_ref=dst, send_sem=send, recv_sem=recv,
        device_id={"row": row, "col": col}, device_id_type=MESH_ID,
    )


def await_bytes(ref, sem):
    pltpu.make_async_copy(ref, ref, sem).wait()


def layer_kernel(
    rows, cols, tok_ref, cot_ref, wg_hbm, wu_hbm, wd_hbm, gm_ref, um_ref, dm_ref, out_ref,
    wg, wu, wd, panel, stage, own, sums, both, acc, pout, land, total,
    w_sem, ch_send, ch_recv, part_send, part_recv, src_send, stage_recv, col_send, col_recv, gather_send, pan_recv, rs_send, rs_recv, fin_send, fin_recv,
):
    row, col = lax.axis_index("row"), lax.axis_index("col")
    last = rows - 1
    per = cols // rows
    chip, core = col // per, col % per
    blocks, _, _, size, feats = panel.shape
    slices, _, width = wg.shape
    subs = blocks // rows
    chunks = blocks * slices
    _, reducers, piece, _ = pout.shape
    split = reducers // (2 * per)
    slab = stage.shape[3]
    relays = size // slab
    parted = part_send.shape[1]

    low = row < rows // 2
    near, far = jnp.where(low, 0, 1), jnp.where(low, 1, 0)
    near_pos, far_pos = jnp.minimum(row, last - row), jnp.maximum(row, last - row)
    near_next = jnp.where(low, row + 1, row - 1)
    far_next = jnp.clip(jnp.where(low, row - 1, row + 1), 0, last)

    def load(j):
        span = pl.ds(pl.multiple_of(j * width, width), width)
        return (
            pltpu.make_async_copy(wg_hbm.at[:, span], wg.at[j], w_sem.at[0, j]),
            pltpu.make_async_copy(wu_hbm.at[:, span], wu.at[j], w_sem.at[1, j]),
            pltpu.make_async_copy(wd_hbm.at[span, :], wd.at[j], w_sem.at[2, j]),
        )

    def load_start(j, carry):
        for copy in load(j):
            copy.start()
        return carry

    lax.fori_loop(0, slices, load_start, 0)

    barrier = pltpu.get_barrier_semaphore()

    def greet(i, carry):
        @pl.when(i != row * cols + col)
        def _():
            pl.semaphore_signal(
                barrier, inc=1, device_id={"row": i // cols, "col": i % cols}, device_id_type=MESH_ID
            )
        return carry

    lax.fori_loop(0, rows * cols, greet, 0)
    pl.semaphore_wait(barrier, rows * cols - 1)

    def prune(j):
        for copy in load(j):
            copy.wait()
        for i in range(wg.shape[1] // BLOCK):
            for n in range(width // BLOCK):
                at = j * (width // BLOCK) + n
                feat, hid = slice(i * BLOCK, (i + 1) * BLOCK), slice(n * BLOCK, (n + 1) * BLOCK)
                wg[j, feat, hid] = wg[j, feat, hid] * jnp.full((BLOCK, BLOCK), gm_ref[i, at].astype(f32)).astype(bf16)
                wu[j, feat, hid] = wu[j, feat, hid] * jnp.full((BLOCK, BLOCK), um_ref[i, at].astype(f32)).astype(bf16)
                wd[j, hid, feat] = wd[j, hid, feat] * jnp.full((BLOCK, BLOCK), dm_ref[i, at].astype(f32)).astype(bf16)

    def rows_of(t, g):
        return pl.ds(pl.multiple_of((t % subs) * size + g * slab, slab), slab)

    def source_copies(t, off):
        g = lax.rem(chip + off, rows)
        return [
            remote(
                ref.at[rows_of(t, g % relays), :], stage.at[t % subs, chip, i], src_send.at[t % subs, off - 1, i],
                stage_recv.at[t % subs, chip], row, g * per + core,
            )
            for i, ref in enumerate((tok_ref, cot_ref))
        ]

    def source(t):
        @pl.when(row == t // subs)
        def _():
            for off in range(1, rows):
                @pl.when(lax.rem(chip + off, rows) < relays)
                def _():
                    for copy in source_copies(t, off):
                        copy.start()

            @pl.when(chip < relays)
            def _():
                stage[t % subs, chip, 0] = tok_ref[rows_of(t, chip % relays), :]
                stage[t % subs, chip, 1] = cot_ref[rows_of(t, chip % relays), :]

    mine = pl.ds(pl.multiple_of((chip % relays) * slab, slab), slab)

    def column_copy(t, a):
        return remote(
            stage.at[t % subs, a], panel.at[t, core, :, mine, :], col_send.at[t % subs, a], col_recv.at[t], a, col
        )

    def relay(t):
        @pl.when((row == t // subs) & (chip < relays))
        def _():
            for off in range(1, rows):
                a = lax.rem(row + off, rows)

                @pl.when(a != chip)
                def _():
                    await_bytes(stage.at[t % subs, a], stage_recv.at[t % subs, a])

                column_copy(t, a).start()

            @pl.when(row != chip)
            def _():
                await_bytes(stage.at[t % subs, row], stage_recv.at[t % subs, row])

            panel[t, core, :, mine, :] = stage[t % subs, row]

    def gather_copy(t, off):
        return remote(
            panel.at[t, core, :, mine, :], panel.at[t, core, :, mine, :], gather_send.at[t, off - 1],
            pan_recv.at[t, core, chip % relays], row, lax.rem(col + off, cols),
        )

    def gather(t):
        @pl.when(chip < relays)
        def _():
            @pl.when(row != t // subs)
            def _():
                await_bytes(panel.at[t, core, :, mine, :], col_recv.at[t])

            for off in range(1, cols):
                gather_copy(t, off).start()

    def arrive(t):
        for h in range(per):
            for g in range(relays):
                @pl.when((core != h) | (chip != g))
                def _():
                    await_bytes(panel.at[t, h, :, g * slab : (g + 1) * slab, :], pan_recv.at[t, h, g])

    def near_copy(k):
        return remote(
            sums.at[near, k], sums.at[near, k], ch_send.at[near, k], ch_recv.at[near, k], near_next, col
        )

    def far_copy(k):
        return remote(sums.at[far, k], sums.at[far, k], ch_send.at[far, k], ch_recv.at[far, k], far_next, col)

    def near_part(k, i):
        k = k % parted
        return remote(
            sums.at[near, k, i], sums.at[near, k, i], part_send.at[near, k, i], part_recv.at[near, k, i], near_next, col
        )

    def far_part(k, i):
        k = k % parted
        return remote(
            sums.at[far, k, i], sums.at[far, k, i], part_send.at[far, k, i], part_recv.at[far, k, i], far_next, col
        )

    def project(k):
        t, j = k // slices, k % slices

        @pl.when((k >= min(EARLY, slices)) & (k < slices))
        def _():
            prune(k)

        @pl.when(j == 0)
        def _():
            arrive(t)

        gate = up = grad = 0.0
        for h in range(per):
            feat = slice(h * feats, (h + 1) * feats)
            tok, cot = panel[t, h, 0], panel[t, h, 1]
            gate += jnp.dot(tok, wg[j, feat, :], preferred_element_type=f32)
            up += jnp.dot(tok, wu[j, feat, :], preferred_element_type=f32)
            grad += lax.dot_general(cot, wd[j, :, feat], CONTRACT, preferred_element_type=f32)
        own[k, 0] = gate
        own[k, 1] = up
        own[k, 2] = grad

    def pass_near(k):
        @pl.when(k < parted)
        def _():
            for i in range(3):
                @pl.when(near_pos == 0)
                def _():
                    sums[near, k, i] = own[k, i].astype(bf16)

                @pl.when(near_pos > 0)
                def _():
                    near_part(k, i).wait_recv()
                    sums[near, k, i] = (own[k, i] + sums[near, k, i].astype(f32)).astype(bf16)

                near_part(k, i).start()

        @pl.when(k >= parted)
        def _():
            @pl.when(near_pos == 0)
            def _():
                sums[near, k] = own[k].astype(bf16)

            @pl.when(near_pos > 0)
            def _():
                near_copy(k).wait_recv()
                sums[near, k] = (own[k] + sums[near, k].astype(f32)).astype(bf16)

            near_copy(k).start()

    def pass_far(k):
        t, j = k // slices, k % slices

        @pl.when(k < parted)
        def _():
            for i in range(3):
                far_part(k, i).wait_recv()
                came = sums[far, k, i].astype(f32)
                both[i] = came + sums[near, k, i].astype(f32)

                @pl.when(far_pos < last)
                def _():
                    sums[far, k, i] = (own[k, i] + came).astype(bf16)
                    far_part(k, i).start()

        @pl.when(k >= parted)
        def _():
            far_copy(k).wait_recv()
            came = sums[far, k].astype(f32)
            both[...] = came + sums[near, k].astype(f32)

            @pl.when(far_pos < last)
            def _():
                sums[far, k] = (own[k] + came).astype(bf16)
                far_copy(k).start()

        gate, up, grad = both[0], both[1], both[2]
        sigma = jax.nn.sigmoid(gate)
        silu = gate * sigma
        hidden = (silu * up).astype(bf16)
        grad_gate = (grad * up * sigma * (1.0 + gate * (1.0 - sigma))).astype(bf16)
        grad_up = (grad * silu).astype(bf16)

        @pl.when(j == 0)
        def _():
            acc[...] = jnp.zeros_like(acc)

        acc[0] += jnp.dot(hidden, wd[j], preferred_element_type=f32)
        acc[1] += lax.dot_general(grad_gate, wg[j], CONTRACT, preferred_element_type=f32) + lax.dot_general(
            grad_up, wu[j], CONTRACT, preferred_element_type=f32
        )

        @pl.when((j == slices // 2) & (t > 0))
        def _():
            combine(t - 1)

        @pl.when(j == slices - 1)
        def _():
            scatter(t)

    def scatter_copy(t, off):
        return remote(
            pout.at[t, lax.rem(col + off, cols) % reducers], land.at[t, cols - 1 - off], rs_send.at[t, off - 1],
            rs_recv.at[t], row, lax.rem(col + off, cols),
        )

    def scatter(t):
        for a in range(2):
            for h in range(per):
                for r in range(split):
                    pout[t, (a * per + h) * split + r] = acc[
                        a, r * piece : (r + 1) * piece, h * feats : (h + 1) * feats
                    ].astype(bf16)
        for off in range(1, cols):
            @pl.when(lax.rem(col + off, cols) < reducers)
            def _():
                scatter_copy(t, off).start()

    part = col % split
    half = (col // split) % per
    which = lax.rem(col // (split * per), 2)
    owner_col = row * per + half

    def give(t):
        span = pl.ds(pl.multiple_of((t % subs) * size + part * piece, piece), piece)
        return remote(
            total.at[t], out_ref.at[which, span, :], fin_send.at[t], fin_recv.at[t % subs, which, part],
            t // subs, owner_col,
        )

    def keep(t):
        span = pl.ds(pl.multiple_of((t % subs) * size + part * piece, piece), piece)
        return pltpu.make_async_copy(total.at[t], out_ref.at[which, span, :], fin_send.at[t])

    def combine(t):
        @pl.when(col < reducers)
        def _():
            await_bytes(land.at[t], rs_recv.at[t])
            value = pout[t, col % reducers].astype(f32)
            for i in range(cols - 1):
                value = value + land[t, i].astype(f32)
            mine = (row == t // subs) & (col == owner_col)

            total[t] = value.astype(bf16)

            @pl.when(mine)
            def _():
                keep(t).start()

            @pl.when(jnp.logical_not(mine) & ((t < blocks - 1 - DEFER) | (t == blocks - 1)))
            def _():
                give(t).start()

    source(row * subs)

    @pl.when(row != 0)
    def _():
        for u in range(1, subs):
            source(row * subs + u)

    relay(0)
    gather(0)

    @pl.when(row == 0)
    def _():
        for u in range(1, subs):
            source(u)

    @pl.when(row != 0)
    def _():
        relay(row * subs)

    for u in range(1, subs):
        relay(row * subs + u)

    for j in range(min(EARLY, slices)):
        prune(j)
    project(0)

    def offset(pos):
        return LAG * pos + jnp.where(pos > 0, HEAD, 0) + jnp.where(pos == last, TAIL, 0)

    def step(s, carry):
        t, j = s // slices, s % slices

        @pl.when((j == GATHER_AT * slices // 8) & (t + 1 < blocks))
        def _():
            gather(t + 1)

        k_near = s - offset(near_pos)
        k_far = s - offset(far_pos)

        def do_near():
            @pl.when((k_near >= 0) & (k_near < chunks))
            def _():
                pass_near(k_near)

        def do_far():
            @pl.when((k_far >= 0) & (k_far < chunks))
            def _():
                pass_far(k_far)

        def do_project():
            @pl.when(s + 1 < chunks)
            def _():
                project(s + 1)

        for do in ((do_near, do_far, do_project), (do_near, do_project, do_far))[ORDER]:
            do()

        return carry

    lax.fori_loop(0, chunks + LAG * last + HEAD + TAIL, step, 0)
    def give_late(t, carry):
        @pl.when((col < reducers) & jnp.logical_not((row == t // subs) & (col == owner_col)))
        def _():
            give(t).start()

        return carry

    lax.fori_loop(max(0, blocks - 1 - DEFER), blocks - 1, give_late, 0)

    for k in range(parted):
        for i in range(3):
            near_part(k, i).wait_send()

            @pl.when(far_pos < last)
            def _():
                far_part(k, i).wait_send()

    def drain_chunk(k, carry):
        near_copy(k).wait_send()

        @pl.when(far_pos < last)
        def _():
            far_copy(k).wait_send()

        return carry

    lax.fori_loop(parted, chunks, drain_chunk, 0)

    def drain_block(t, carry):
        @pl.when(row == t // subs)
        def _():
            for off in range(1, rows):
                @pl.when(lax.rem(chip + off, rows) < relays)
                def _():
                    for copy in source_copies(t, off):
                        copy.wait_send()

        @pl.when((row == t // subs) & (chip < relays))
        def _():
            for off in range(1, rows):
                column_copy(t, lax.rem(row + off, rows)).wait_send()

        @pl.when(chip < relays)
        def _():
            for off in range(1, cols):
                gather_copy(t, off).wait_send()

        return carry

    lax.fori_loop(0, blocks, drain_block, 0)
    combine(blocks - 1)

    def drain_collect(t, carry):
        for off in range(1, cols):
            @pl.when(lax.rem(col + off, cols) < reducers)
            def _():
                scatter_copy(t, off).wait_send()

        @pl.when((col < reducers) & jnp.logical_not((row == t // subs) & (col == owner_col)))
        def _():
            give(t).wait_send()

        @pl.when((row == t // subs) & (col == owner_col) & (col < reducers))
        def _():
            keep(t).wait()

        return carry

    lax.fori_loop(0, blocks, drain_collect, 0)

    for s in range(subs):
        for a in range(2):
            for r in range(split):
                @pl.when((row != chip) | (col != (a * per + core) * split + r))
                def _():
                    start = s * size + r * piece
                    await_bytes(out_ref.at[a, start : start + piece, :], fin_recv.at[s, a, r])


def unstack_kernel(pair_ref, out_ref, grad_ref):
    out_ref[...] = pair_ref[0]
    grad_ref[...] = pair_ref[1]


def body(tokens, cotangent, gate_weight, up_weight, down_weight, gate_mask, up_mask, down_mask):
    rows, cols = lax.axis_size("row"), lax.axis_size("col")
    per = cols // rows
    local_tokens, feats = tokens.shape
    depth, hidden = gate_weight.shape
    size = min(TOKEN_BLOCK, local_tokens)
    width = min(WIDTH, hidden)
    slices = hidden // width
    subs = local_tokens // size
    blocks = rows * subs
    chunks = blocks * slices
    split = max(1, min(cols // (2 * per), size // 16))
    reducers = 2 * per * split
    piece = size // split
    relays = max(1, min(rows, size // 16))
    dma = pltpu.SemaphoreType.DMA
    vmem = pl.BlockSpec(memory_space=pltpu.VMEM)
    smem = pl.BlockSpec(memory_space=pltpu.SMEM)
    hbm = pl.BlockSpec(memory_space=pl.ANY)
    shard = jax.ShapeDtypeStruct((local_tokens, feats), bf16)
    pair = pl.pallas_call(
        functools.partial(layer_kernel, rows, cols),
        out_shape=jax.ShapeDtypeStruct((2, local_tokens, feats), bf16),
        in_specs=[vmem, vmem, hbm, hbm, hbm, smem, smem, smem],
        out_specs=hbm,
        scratch_shapes=[
            pltpu.VMEM((slices, depth, width), bf16),
            pltpu.VMEM((slices, depth, width), bf16),
            pltpu.VMEM((slices, width, depth), bf16),
            pltpu.VMEM((blocks, per, 2, size, feats), bf16),
            pltpu.VMEM((subs, rows, 2, size // relays, feats), bf16),
            pltpu.VMEM((chunks, 3, size, width), f32),
            pltpu.VMEM((2, chunks, 3, size, width), bf16),
            pltpu.VMEM((3, size, width), f32),
            pltpu.VMEM((2, size, depth), f32),
            pltpu.VMEM((blocks, reducers, piece, feats), bf16),
            pltpu.VMEM((blocks, cols - 1, piece, feats), bf16),
            pltpu.VMEM((blocks, piece, feats), bf16),
            dma((3, slices)),
            dma((2, chunks)),
            dma((2, chunks)),
            dma((2, min(PARTED, chunks), 3)),
            dma((2, min(PARTED, chunks), 3)),
            dma((subs, rows - 1, 2)),
            dma((subs, rows)),
            dma((subs, rows)),
            dma((blocks,)),
            dma((blocks, cols - 1)),
            dma((blocks, per, relays)),
            dma((blocks, cols - 1)),
            dma((blocks,)),
            dma((blocks,)),
            dma((subs, 2, split)),
        ],
        compiler_params=pltpu.CompilerParams(
            collective_id=0, has_side_effects=True, vmem_limit_bytes=58 * 1024 * 1024
        ),
        name="layer",
    )(tokens, cotangent, gate_weight, up_weight, down_weight, gate_mask, up_mask, down_mask.T)
    return pl.pallas_call(
        unstack_kernel, out_shape=(shard, shard), in_specs=[vmem], out_specs=(vmem, vmem), name="unstack"
    )(pair)


def solution(mesh):
    in_specs = (
        P("row", "col"),
        P("row", "col"),
        P("row", "col"),
        P("row", "col"),
        P("col", "row"),
        P("row", "col"),
        P("row", "col"),
        P("col", "row"),
    )
    out_specs = (P("row", "col"), P("row", "col"))
    return jax.shard_map(body, mesh=mesh, in_specs=in_specs, out_specs=out_specs, check_vma=False)
```

```python
import functools

import jax
import jax.numpy as jnp
from jax import lax
from jax.experimental import pallas as pl
from jax.experimental.pallas import tpu as pltpu
from jax.sharding import PartitionSpec as P

BLOCK = 128
TOKEN_BLOCK = 64
WIDTH = 256
LAG = 3
HEAD = 0
TAIL = 0
ORDER = 1
PARTED = 2
EARLY = 3
GATHER_AT = 3
DEFER = 3
CONTRACT = (((1,), (1,)), ((), ()))
MESH_ID = pl.DeviceIdType.MESH
bf16, f32 = jnp.bfloat16, jnp.float32


def remote(src, dst, send, recv, row, col):
    return pltpu.make_async_remote_copy(
        src_ref=src, dst_ref=dst, send_sem=send, recv_sem=recv,
        device_id={"row": row, "col": col}, device_id_type=MESH_ID,
    )


def await_bytes(ref, sem):
    pltpu.make_async_copy(ref, ref, sem).wait()


def layer_kernel(
    rows, cols, tok_ref, cot_ref, wg_hbm, wu_hbm, wd_hbm, gm_ref, um_ref, dm_ref, out_ref,
    wg, wu, wd, panel, stage, own, sums, both, acc, pout, land, total,
    w_sem, ch_send, ch_recv, part_send, part_recv, src_send, stage_recv, col_send, col_recv, gather_send, pan_recv, rs_send, rs_recv, fin_send, fin_recv,
):
    row, col = lax.axis_index("row"), lax.axis_index("col")
    last = rows - 1
    per = cols // rows
    chip, core = col // per, col % per
    blocks, _, _, size, feats = panel.shape
    slices, _, width = wg.shape
    subs = blocks // rows
    chunks = blocks * slices
    _, reducers, piece, _ = pout.shape
    split = reducers // (2 * per)
    slab = stage.shape[3]
    relays = size // slab
    parted = part_send.shape[1]

    low = row < rows // 2
    near, far = jnp.where(low, 0, 1), jnp.where(low, 1, 0)
    near_pos, far_pos = jnp.minimum(row, last - row), jnp.maximum(row, last - row)
    near_next = jnp.where(low, row + 1, row - 1)
    far_next = jnp.clip(jnp.where(low, row - 1, row + 1), 0, last)

    def load(j):
        span = pl.ds(pl.multiple_of(j * width, width), width)
        return (
            pltpu.make_async_copy(wg_hbm.at[:, span], wg.at[j], w_sem.at[0, j]),
            pltpu.make_async_copy(wu_hbm.at[:, span], wu.at[j], w_sem.at[1, j]),
            pltpu.make_async_copy(wd_hbm.at[span, :], wd.at[j], w_sem.at[2, j]),
        )

    def load_start(j, carry):
        for copy in load(j):
            copy.start()
        return carry

    lax.fori_loop(0, slices, load_start, 0)

    barrier = pltpu.get_barrier_semaphore()

    def greet(i, carry):
        @pl.when(i != row * cols + col)
        def _():
            pl.semaphore_signal(
                barrier, inc=1, device_id={"row": i // cols, "col": i % cols}, device_id_type=MESH_ID
            )
        return carry

    lax.fori_loop(0, rows * cols, greet, 0)
    pl.semaphore_wait(barrier, rows * cols - 1)

    def prune(j):
        for copy in load(j):
            copy.wait()
        for i in range(wg.shape[1] // BLOCK):
            for n in range(width // BLOCK):
                at = j * (width // BLOCK) + n
                feat, hid = slice(i * BLOCK, (i + 1) * BLOCK), slice(n * BLOCK, (n + 1) * BLOCK)
                wg[j, feat, hid] = wg[j, feat, hid] * jnp.full((BLOCK, BLOCK), gm_ref[i, at].astype(f32)).astype(bf16)
                wu[j, feat, hid] = wu[j, feat, hid] * jnp.full((BLOCK, BLOCK), um_ref[i, at].astype(f32)).astype(bf16)
                wd[j, hid, feat] = wd[j, hid, feat] * jnp.full((BLOCK, BLOCK), dm_ref[i, at].astype(f32)).astype(bf16)

    def rows_of(t, g):
        return pl.ds(pl.multiple_of((t % subs) * size + g * slab, slab), slab)

    def source_copies(t, off):
        g = lax.rem(chip + off, rows)
        return [
            remote(
                ref.at[rows_of(t, g % relays), :], stage.at[t % subs, chip, i], src_send.at[t % subs, off - 1, i],
                stage_recv.at[t % subs, chip], row, g * per + core,
            )
            for i, ref in enumerate((tok_ref, cot_ref))
        ]

    def source(t):
        @pl.when(row == t // subs)
        def _():
            for off in range(1, rows):
                @pl.when(lax.rem(chip + off, rows) < relays)
                def _():
                    for copy in source_copies(t, off):
                        copy.start()

            @pl.when(chip < relays)
            def _():
                stage[t % subs, chip, 0] = tok_ref[rows_of(t, chip % relays), :]
                stage[t % subs, chip, 1] = cot_ref[rows_of(t, chip % relays), :]

    mine = pl.ds(pl.multiple_of((chip % relays) * slab, slab), slab)

    def column_copy(t, a):
        return remote(
            stage.at[t % subs, a], panel.at[t, core, :, mine, :], col_send.at[t % subs, a], col_recv.at[t], a, col
        )

    def relay(t):
        @pl.when((row == t // subs) & (chip < relays))
        def _():
            for off in range(1, rows):
                a = lax.rem(row + off, rows)

                @pl.when(a != chip)
                def _():
                    await_bytes(stage.at[t % subs, a], stage_recv.at[t % subs, a])

                column_copy(t, a).start()

            @pl.when(row != chip)
            def _():
                await_bytes(stage.at[t % subs, row], stage_recv.at[t % subs, row])

            panel[t, core, :, mine, :] = stage[t % subs, row]

    def gather_copy(t, off):
        return remote(
            panel.at[t, core, :, mine, :], panel.at[t, core, :, mine, :], gather_send.at[t, off - 1],
            pan_recv.at[t, core, chip % relays], row, lax.rem(col + off, cols),
        )

    def gather(t):
        @pl.when(chip < relays)
        def _():
            @pl.when(row != t // subs)
            def _():
                await_bytes(panel.at[t, core, :, mine, :], col_recv.at[t])

            for off in range(1, cols):
                gather_copy(t, off).start()

    def arrive(t):
        for h in range(per):
            for g in range(relays):
                @pl.when((core != h) | (chip != g))
                def _():
                    await_bytes(panel.at[t, h, :, g * slab : (g + 1) * slab, :], pan_recv.at[t, h, g])

    def near_copy(k):
        return remote(
            sums.at[near, k], sums.at[near, k], ch_send.at[near, k], ch_recv.at[near, k], near_next, col
        )

    def far_copy(k):
        return remote(sums.at[far, k], sums.at[far, k], ch_send.at[far, k], ch_recv.at[far, k], far_next, col)

    def near_part(k, i):
        k = k % parted
        return remote(
            sums.at[near, k, i], sums.at[near, k, i], part_send.at[near, k, i], part_recv.at[near, k, i], near_next, col
        )

    def far_part(k, i):
        k = k % parted
        return remote(
            sums.at[far, k, i], sums.at[far, k, i], part_send.at[far, k, i], part_recv.at[far, k, i], far_next, col
        )

    def project(k):
        t, j = k // slices, k % slices

        @pl.when((k >= min(EARLY, slices)) & (k < slices))
        def _():
            prune(k)

        @pl.when(j == 0)
        def _():
            arrive(t)

        gate = up = grad = 0.0
        for h in range(per):
            feat = slice(h * feats, (h + 1) * feats)
            tok, cot = panel[t, h, 0], panel[t, h, 1]
            gate += jnp.dot(tok, wg[j, feat, :], preferred_element_type=f32)
            up += jnp.dot(tok, wu[j, feat, :], preferred_element_type=f32)
            grad += lax.dot_general(cot, wd[j, :, feat], CONTRACT, preferred_element_type=f32)
        own[k, 0] = gate
        own[k, 1] = up
        own[k, 2] = grad

    def pass_near(k):
        @pl.when(k < parted)
        def _():
            for i in range(3):
                @pl.when(near_pos == 0)
                def _():
                    sums[near, k, i] = own[k, i].astype(bf16)

                @pl.when(near_pos > 0)
                def _():
                    near_part(k, i).wait_recv()
                    sums[near, k, i] = (own[k, i] + sums[near, k, i].astype(f32)).astype(bf16)

                near_part(k, i).start()

        @pl.when(k >= parted)
        def _():
            @pl.when(near_pos == 0)
            def _():
                sums[near, k] = own[k].astype(bf16)

            @pl.when(near_pos > 0)
            def _():
                near_copy(k).wait_recv()
                sums[near, k] = (own[k] + sums[near, k].astype(f32)).astype(bf16)

            near_copy(k).start()

    def pass_far(k):
        t, j = k // slices, k % slices

        @pl.when(k < parted)
        def _():
            for i in range(3):
                far_part(k, i).wait_recv()
                came = sums[far, k, i].astype(f32)
                both[i] = came + sums[near, k, i].astype(f32)

                @pl.when(far_pos < last)
                def _():
                    sums[far, k, i] = (own[k, i] + came).astype(bf16)
                    far_part(k, i).start()

        @pl.when(k >= parted)
        def _():
            far_copy(k).wait_recv()
            came = sums[far, k].astype(f32)
            both[...] = came + sums[near, k].astype(f32)

            @pl.when(far_pos < last)
            def _():
                sums[far, k] = (own[k] + came).astype(bf16)
                far_copy(k).start()

        gate, up, grad = both[0], both[1], both[2]
        sigma = jax.nn.sigmoid(gate)
        silu = gate * sigma
        hidden = (silu * up).astype(bf16)
        grad_gate = (grad * up * sigma * (1.0 + gate * (1.0 - sigma))).astype(bf16)
        grad_up = (grad * silu).astype(bf16)

        @pl.when(j == 0)
        def _():
            acc[...] = jnp.zeros_like(acc)

        acc[0] += jnp.dot(hidden, wd[j], preferred_element_type=f32)

        @pl.when(j == slices - 1)
        def _():
            scatter(t, 0)

        acc[1] += lax.dot_general(grad_gate, wg[j], CONTRACT, preferred_element_type=f32) + lax.dot_general(
            grad_up, wu[j], CONTRACT, preferred_element_type=f32
        )

        @pl.when((j == slices // 2) & (t > 0))
        def _():
            combine(t - 1)

        @pl.when(j == slices - 1)
        def _():
            scatter(t, 1)

    def scatter_copy(t, off):
        return remote(
            pout.at[t, lax.rem(col + off, cols) % reducers], land.at[t, cols - 1 - off], rs_send.at[t, off - 1],
            rs_recv.at[t], row, lax.rem(col + off, cols),
        )

    def scatter(t, a):
        for h in range(per):
            for r in range(split):
                pout[t, (a * per + h) * split + r] = acc[
                    a, r * piece : (r + 1) * piece, h * feats : (h + 1) * feats
                ].astype(bf16)
        for off in range(1, cols):
            @pl.when(lax.rem(col + off, cols) // (per * split) == a)
            def _():
                scatter_copy(t, off).start()

    part = col % split
    half = (col // split) % per
    which = lax.rem(col // (split * per), 2)
    owner_col = row * per + half

    def give(t):
        span = pl.ds(pl.multiple_of((t % subs) * size + part * piece, piece), piece)
        return remote(
            total.at[t], out_ref.at[which, span, :], fin_send.at[t], fin_recv.at[t % subs, which, part],
            t // subs, owner_col,
        )

    def keep(t):
        span = pl.ds(pl.multiple_of((t % subs) * size + part * piece, piece), piece)
        return pltpu.make_async_copy(total.at[t], out_ref.at[which, span, :], fin_send.at[t])

    def combine(t):
        @pl.when(col < reducers)
        def _():
            await_bytes(land.at[t], rs_recv.at[t])
            value = pout[t, col % reducers].astype(f32)
            for i in range(cols - 1):
                value = value + land[t, i].astype(f32)
            mine = (row == t // subs) & (col == owner_col)

            total[t] = value.astype(bf16)

            @pl.when(mine)
            def _():
                keep(t).start()

            @pl.when(jnp.logical_not(mine) & ((t < blocks - 1 - DEFER) | (t == blocks - 1)))
            def _():
                give(t).start()

    source(row * subs)

    @pl.when(row != 0)
    def _():
        for u in range(1, subs):
            source(row * subs + u)

    relay(0)
    gather(0)

    @pl.when(row == 0)
    def _():
        for u in range(1, subs):
            source(u)

    @pl.when(row != 0)
    def _():
        relay(row * subs)

    for u in range(1, subs):
        relay(row * subs + u)

    for j in range(min(EARLY, slices)):
        prune(j)
    project(0)

    def offset(pos):
        return LAG * pos + jnp.where(pos > 0, HEAD, 0) + jnp.where(pos == last, TAIL, 0)

    def step(s, carry):
        t, j = s // slices, s % slices

        @pl.when((j == GATHER_AT * slices // 8) & (t + 1 < blocks))
        def _():
            gather(t + 1)

        k_near = s - offset(near_pos)
        k_far = s - offset(far_pos)

        def do_near():
            @pl.when((k_near >= 0) & (k_near < chunks))
            def _():
                pass_near(k_near)

        def do_far():
            @pl.when((k_far >= 0) & (k_far < chunks))
            def _():
                pass_far(k_far)

        def do_project():
            @pl.when(s + 1 < chunks)
            def _():
                project(s + 1)

        for do in ((do_near, do_far, do_project), (do_near, do_project, do_far))[ORDER]:
            do()

        return carry

    lax.fori_loop(0, chunks + LAG * last + HEAD + TAIL, step, 0)
    def give_late(t, carry):
        @pl.when((col < reducers) & jnp.logical_not((row == t // subs) & (col == owner_col)))
        def _():
            give(t).start()

        return carry

    lax.fori_loop(max(0, blocks - 1 - DEFER), blocks - 1, give_late, 0)

    for k in range(parted):
        for i in range(3):
            near_part(k, i).wait_send()

            @pl.when(far_pos < last)
            def _():
                far_part(k, i).wait_send()

    def drain_chunk(k, carry):
        near_copy(k).wait_send()

        @pl.when(far_pos < last)
        def _():
            far_copy(k).wait_send()

        return carry

    lax.fori_loop(parted, chunks, drain_chunk, 0)

    def drain_block(t, carry):
        @pl.when(row == t // subs)
        def _():
            for off in range(1, rows):
                @pl.when(lax.rem(chip + off, rows) < relays)
                def _():
                    for copy in source_copies(t, off):
                        copy.wait_send()

        @pl.when((row == t // subs) & (chip < relays))
        def _():
            for off in range(1, rows):
                column_copy(t, lax.rem(row + off, rows)).wait_send()

        @pl.when(chip < relays)
        def _():
            for off in range(1, cols):
                gather_copy(t, off).wait_send()

        return carry

    lax.fori_loop(0, blocks, drain_block, 0)
    combine(blocks - 1)

    def drain_collect(t, carry):
        for off in range(1, cols):
            @pl.when(lax.rem(col + off, cols) < reducers)
            def _():
                scatter_copy(t, off).wait_send()

        @pl.when((col < reducers) & jnp.logical_not((row == t // subs) & (col == owner_col)))
        def _():
            give(t).wait_send()

        @pl.when((row == t // subs) & (col == owner_col) & (col < reducers))
        def _():
            keep(t).wait()

        return carry

    lax.fori_loop(0, blocks, drain_collect, 0)

    for s in range(subs):
        for a in range(2):
            for r in range(split):
                @pl.when((row != chip) | (col != (a * per + core) * split + r))
                def _():
                    start = s * size + r * piece
                    await_bytes(out_ref.at[a, start : start + piece, :], fin_recv.at[s, a, r])


def unstack_kernel(pair_ref, out_ref, grad_ref):
    out_ref[...] = pair_ref[0]
    grad_ref[...] = pair_ref[1]


def body(tokens, cotangent, gate_weight, up_weight, down_weight, gate_mask, up_mask, down_mask):
    rows, cols = lax.axis_size("row"), lax.axis_size("col")
    per = cols // rows
    local_tokens, feats = tokens.shape
    depth, hidden = gate_weight.shape
    size = min(TOKEN_BLOCK, local_tokens)
    width = min(WIDTH, hidden)
    slices = hidden // width
    subs = local_tokens // size
    blocks = rows * subs
    chunks = blocks * slices
    split = max(1, min(cols // (2 * per), size // 16))
    reducers = 2 * per * split
    piece = size // split
    relays = max(1, min(rows, size // 16))
    dma = pltpu.SemaphoreType.DMA
    vmem = pl.BlockSpec(memory_space=pltpu.VMEM)
    smem = pl.BlockSpec(memory_space=pltpu.SMEM)
    hbm = pl.BlockSpec(memory_space=pl.ANY)
    shard = jax.ShapeDtypeStruct((local_tokens, feats), bf16)
    pair = pl.pallas_call(
        functools.partial(layer_kernel, rows, cols),
        out_shape=jax.ShapeDtypeStruct((2, local_tokens, feats), bf16),
        in_specs=[vmem, vmem, hbm, hbm, hbm, smem, smem, smem],
        out_specs=hbm,
        scratch_shapes=[
            pltpu.VMEM((slices, depth, width), bf16),
            pltpu.VMEM((slices, depth, width), bf16),
            pltpu.VMEM((slices, width, depth), bf16),
            pltpu.VMEM((blocks, per, 2, size, feats), bf16),
            pltpu.VMEM((subs, rows, 2, size // relays, feats), bf16),
            pltpu.VMEM((chunks, 3, size, width), f32),
            pltpu.VMEM((2, chunks, 3, size, width), bf16),
            pltpu.VMEM((3, size, width), f32),
            pltpu.VMEM((2, size, depth), f32),
            pltpu.VMEM((blocks, reducers, piece, feats), bf16),
            pltpu.VMEM((blocks, cols - 1, piece, feats), bf16),
            pltpu.VMEM((blocks, piece, feats), bf16),
            dma((3, slices)),
            dma((2, chunks)),
            dma((2, chunks)),
            dma((2, min(PARTED, chunks), 3)),
            dma((2, min(PARTED, chunks), 3)),
            dma((subs, rows - 1, 2)),
            dma((subs, rows)),
            dma((subs, rows)),
            dma((blocks,)),
            dma((blocks, cols - 1)),
            dma((blocks, per, relays)),
            dma((blocks, cols - 1)),
            dma((blocks,)),
            dma((blocks,)),
            dma((subs, 2, split)),
        ],
        compiler_params=pltpu.CompilerParams(
            collective_id=0, has_side_effects=True, vmem_limit_bytes=58 * 1024 * 1024
        ),
        name="layer",
    )(tokens, cotangent, gate_weight, up_weight, down_weight, gate_mask, up_mask, down_mask.T)
    return pl.pallas_call(
        unstack_kernel, out_shape=(shard, shard), in_specs=[vmem], out_specs=(vmem, vmem), name="unstack"
    )(pair)


def solution(mesh):
    in_specs = (
        P("row", "col"),
        P("row", "col"),
        P("row", "col"),
        P("row", "col"),
        P("col", "row"),
        P("row", "col"),
        P("row", "col"),
        P("col", "row"),
    )
    out_specs = (P("row", "col"), P("row", "col"))
    return jax.shard_map(body, mesh=mesh, in_specs=in_specs, out_specs=out_specs, check_vma=False)
```
